256 devices in a mesh: req: 4 (over z_hi, core), ctx: 64 (over x, y, z_lo).
Axes of the slice: x: 4, y: 4, z: 8 (z_hi: 2, z_lo: 4; z = z_hi * 4 + z_lo), core: 2. Of those that a mesh axis runs over, the one named last changes fastest.
Arguments:
- query_rows: bfloat16 [4, 7168, 2048], P('req', 'ctx'), may hold values from -120 to 120
- key_rows: bfloat16 [4, 7168, 1024], P('req', 'ctx'), may hold values from -8 to 8
- value_rows: bfloat16 [4, 7168, 1024], P('req', 'ctx'), may hold values from -6 to 6
- image_starts: int32 [4, 14], P('req'), may hold values from 0 to 6912, as said below
- image_counts: int32 [4], P('req'), may hold values from 1 to 14, as said below
Outputs:
- attended: bfloat16 [4, 7168, 2048], P('req', 'ctx')
The draws below stay inside these ranges and needn't reach their ends.
Inputs may be any that keep to these rules, and one draw needn't show every extreme that they name: `image_starts`: each request's row holds 14 distinct multiples of 256 in ascending order, always starting with 0; in some request the last entry is (27) * 256; only the first image_counts entries of a request are image blocks. `image_counts`: some request has 14 image blocks.
All inputs are finite; a program needn't handle non-finite values.
Results may differ from the reference program's by a relative error of at most 0.0059.
Values may be sent and summed in bfloat16 or wider, within the bound.
A program may use at most 128 MiB of HBM per device.

```python
import math
import jax
import jax.numpy as jnp
from jax import lax

HEADS = 16
KV_HEADS = 8
HEAD_DIM = 128
IMG = 256
REQS = 4
SEQ = 7168
SLOTS = 28
MAXIMG = 14


def paired_draw(key):
    base = jax.random.fold_in(key, 11)
    first = jax.random.fold_in(base, 0)
    second = jax.random.fold_in(base, 1)
    third = jax.random.fold_in(base, 2)
    fourth = jax.random.fold_in(base, 3)
    sixth = jax.random.fold_in(base, 5)
    seventh = jax.random.fold_in(base, 6)
    raw_keys = jnp.clip(jax.random.normal(first, (REQS, SEQ, KV_HEADS, HEAD_DIM), jnp.float32), -4.0, 4.0)
    raw_queries = jnp.clip(jax.random.normal(second, (REQS, SEQ, HEADS, HEAD_DIM), jnp.float32), -4.0, 4.0)
    key_scale = jnp.exp(jax.random.uniform(third, (REQS, SEQ, KV_HEADS, 1), jnp.float32, jnp.log(0.2), jnp.log(2.0)))
    query_scale = jnp.exp(jax.random.uniform(fourth, (REQS, SEQ, 1, 1), jnp.float32, jnp.log(0.3), jnp.log(3.0)))
    target = jax.random.uniform(sixth, (REQS, SEQ), jnp.float32) < 1.0 / 64.0
    strong = jax.random.randint(seventh, (REQS, SEQ), 0, KV_HEADS)
    head_index = jnp.arange(KV_HEADS)
    planted_scale = jnp.where(head_index[None, None, :] == strong[:, :, None], 1.2, 0.1).astype(jnp.float32)[..., None]
    planted = raw_keys * planted_scale
    key_out = jnp.where(target[:, :, None, None], planted, raw_keys * key_scale)
    aimed = jnp.roll(target, 421, axis=1)
    source = jnp.repeat(jnp.roll(raw_keys, 421, axis=1), HEADS // KV_HEADS, axis=2)
    strength = 4.0
    query_out = jnp.where(aimed[:, :, None, None], strength * source, raw_queries * query_scale)
    return (query_out.reshape(REQS, SEQ, HEADS * HEAD_DIM), key_out.reshape(REQS, SEQ, KV_HEADS * HEAD_DIM))


def draw_query_rows(key, part):
    return paired_draw(key)[0].astype(jnp.bfloat16)


def draw_key_rows(key, part):
    return paired_draw(key)[1].astype(jnp.bfloat16)


def draw_image_starts(key, part):
    base = jax.random.fold_in(key, 3)
    chosen = jax.random.randint(jax.random.fold_in(base, 1000), (), 0, REQS)

    def one_request(index):
        priority = jax.random.permutation(jax.random.fold_in(base, index), SLOTS - 1).astype(jnp.int32)
        slot_index = jnp.arange(SLOTS - 1, dtype=jnp.int32)
        priority = jnp.where((index == chosen) & (slot_index == SLOTS - 2), SLOTS, priority)
        order = jnp.argsort(-priority, stable=True).astype(jnp.int32) + 1
        picked = jnp.concatenate([jnp.zeros((1,), jnp.int32), order[:MAXIMG - 1]])
        return jnp.sort(picked) * IMG
    return jax.vmap(one_request)(jnp.arange(REQS)).astype(jnp.int32)


def draw_image_counts(key, part):
    first, second, third = jax.random.split(jax.random.fold_in(key, 5), 3)
    lower = jax.random.randint(first, (REQS,), 0, MAXIMG + 1)
    upper = jax.random.randint(second, (REQS,), 0, MAXIMG + 1)
    counts = jnp.minimum(1 + lower * upper // MAXIMG, MAXIMG)
    chosen = jax.random.randint(third, (), 0, REQS)
    return jnp.where(jnp.arange(REQS) == chosen, MAXIMG, counts).astype(jnp.int32)


def block_levels(stream_key, extent, cuts, smallest, high):
    gain = 1.0
    for axis_at, parts in cuts:
        draws = jax.random.uniform(jax.random.fold_in(jax.random.fold_in(stream_key, 6), axis_at), (parts,), jnp.float32, smallest / len(cuts), high / len(cuts))
        gain = gain * jnp.repeat(jnp.exp(draws), extent[axis_at] // parts).reshape((-1,) + (1,) * (len(extent) - 1 - axis_at))
    return gain


def noise(own_key, shape, width, most, pieces=(), kind=jnp.bfloat16):
    loudness = block_levels(own_key, shape, pieces, -0.22, 0.18) if pieces else 1.0
    entries = jax.random.normal(own_key, shape, jnp.float32) * width * loudness
    return jnp.minimum(jnp.maximum(entries, -most), most).astype(kind)


def setup_inputs(seed: int = 0) -> dict:
    streams_of = jax.random.split(jax.random.key(seed), 6)
    return {
        "query_rows": draw_query_rows(jax.random.fold_in(streams_of[5], 71), 0),
        "key_rows": draw_key_rows(jax.random.fold_in(streams_of[5], 71), 0),
        "value_rows": noise(streams_of[2], (REQS, SEQ, KV_HEADS * HEAD_DIM), 1.0, 6.0, ((0, 4), (1, 64))),
        "image_starts": draw_image_starts(jax.random.fold_in(streams_of[5], 71), 0),
        "image_counts": draw_image_counts(jax.random.fold_in(streams_of[5], 71), 0),
    }


score_scale = 168.0 ** -0.5


def image_ids(position, starts, count):
    index = jnp.arange(starts.shape[0], dtype=jnp.int32)
    inside = (starts[None, :] <= position[:, None]) & (position[:, None] < starts[None, :] + IMG) & (index[None, :] < count)
    return (jnp.sum(jnp.where(inside, index[None, :] + 1, 0), axis=1) - 1).astype(jnp.int32)


def reference(query_rows, key_rows, value_rows, image_starts, image_counts):
    block_rows = math.gcd(SEQ, 512)
    block_total = SEQ // block_rows
    group = HEADS // KV_HEADS
    position = jnp.arange(SEQ, dtype=jnp.int32)

    def one_request(items):
        queries, keys, values, starts, count = items
        key_all = keys.reshape(SEQ, KV_HEADS, HEAD_DIM).astype(jnp.float32)
        value_all = values.reshape(SEQ, KV_HEADS, HEAD_DIM).astype(jnp.float32)
        key_ids = image_ids(position, starts, count)

        def one_block(block_index):
            first = (block_index * block_rows).astype(jnp.int32)
            query_block = lax.dynamic_slice_in_dim(queries, first, block_rows, 0)
            query_block = query_block.reshape(block_rows, KV_HEADS, group, HEAD_DIM).astype(jnp.float32)
            query_pos = first + jnp.arange(block_rows, dtype=jnp.int32)
            query_ids = lax.dynamic_slice_in_dim(key_ids, first, block_rows, 0)
            visible = (position[None, :] <= query_pos[:, None]) | ((key_ids[None, :] == query_ids[:, None]) & (query_ids[:, None] >= 0))
            scores = jnp.einsum('qkgd,skd->kgqs', query_block, key_all) * score_scale
            scores = jnp.where(visible[None, None], scores, -jnp.inf)
            largest = jnp.max(scores, axis=-1, keepdims=True)
            weights = jnp.where(visible[None, None], jnp.exp(scores - largest), 0.0)
            total = jnp.sum(weights, axis=-1)
            rounded = lax.optimization_barrier(weights.astype(jnp.bfloat16)).astype(jnp.float32)
            output = jnp.einsum('kgqs,skd->kgqd', rounded, value_all) / total[..., None]
            return output.transpose(2, 0, 1, 3).reshape(block_rows, HEADS * HEAD_DIM).astype(jnp.bfloat16)

        blocks = lax.map(one_block, jnp.arange(block_total, dtype=jnp.int32))
        return blocks.reshape(SEQ, HEADS * HEAD_DIM)

    return lax.map(one_request, (query_rows, key_rows, value_rows, image_starts, image_counts))
```

```python
import functools
import math

import jax
import jax.numpy as jnp
from jax import lax
from jax.experimental import pallas as pl
from jax.experimental.pallas import tpu as pltpu
from jax.sharding import PartitionSpec as P

HEADS = 16
KV_HEADS = 8
HEAD_DIM = 128
IMG = 256
SIDE = 4
PLANE = SIDE * SIDE
GROUP = HEADS // KV_HEADS
WIDE = GROUP * HEAD_DIM
NEG = -1e30
MESH = pl.DeviceIdType.MESH

score_scale = 168.0 ** (-0.5)
EXP2_SCALE = score_scale * math.log2(math.e)


def place(x, y, z):
    return {"ctx": x * PLANE + y * SIDE + z}


def kernel(starts_ref, count_ref, q_ref, k_ref, v_ref, out_ref,
           qg, kv, lim, acc, mx, sm, osend, ssend, orecv, srecv,
           q_ss, q_rs, p_ss, p_rs, up_ss, dn_ss, z_rs, o_ss, o_rs, s_ss, s_rs):
    rows = q_ref.shape[0]
    maximg = starts_ref.shape[1]
    c = lax.axis_index("ctx")
    x, y, z = c // PLANE, (c // SIDE) % SIDE, c % SIDE
    half = ((y + 1) // 2) % 2
    hb = y // 2
    mine = x * SIDE + y

    barrier = pltpu.get_barrier_semaphore()
    for dx in range(SIDE):
        for dy in range(SIDE):
            if dx or dy:
                pl.semaphore_signal(barrier, inc=1, device_id=place((x + dx) % SIDE, (y + dy) % SIDE, z), device_id_type=MESH)

    @pl.when(z < SIDE - 1)
    def _():
        pl.semaphore_signal(barrier, inc=1, device_id=place(x, y, z + 1), device_id_type=MESH)

    @pl.when(z > 0)
    def _():
        pl.semaphore_signal(barrier, inc=1, device_id=place(x, y, z - 1), device_id_type=MESH)

    inner = ((z > 0) & (z < SIDE - 1)).astype(jnp.int32)
    pl.semaphore_wait(barrier, PLANE - 1 + 1 + inner)

    def cols(n, width):
        return pl.ds(pl.multiple_of(n * width, width), width)

    p_sends = []
    for dx in range(SIDE):
        for j in range(2):
            tx = (x + dx) % SIDE
            ty = y if j == 0 else SIDE - 1 - y
            th = 2 * tx + (hb if j == 0 else 1 - hb)
            for t, ref in enumerate((k_ref, v_ref)):
                src = ref.at[:, cols(th, HEAD_DIM)]
                dst = kv.at[x, t, hb, z]
                n = (dx * 2 + j) * 2 + t
                if dx == 0 and j == 0:
                    pltpu.make_async_copy(src, dst, p_rs.at[t, x, hb]).start()
                else:
                    copy = pltpu.make_async_remote_copy(
                        src_ref=src, dst_ref=dst, send_sem=p_ss.at[n], recv_sem=p_rs.at[t, x, hb],
                        device_id=place(tx, ty, z), device_id_type=MESH)
                    copy.start()
                    p_sends.append(copy)
    q_sends = []
    for dx in range(SIDE):
        for dy in range(SIDE):
            tx, ty = (x + dx) % SIDE, (y + dy) % SIDE
            th = 2 * tx + ty // 2
            src = q_ref.at[:, cols(th, WIDE)]
            dst = qg.at[mine]
            if dx == 0 and dy == 0:
                pltpu.make_async_copy(src, dst, q_rs.at[mine]).start()
            else:
                copy = pltpu.make_async_remote_copy(
                    src_ref=src, dst_ref=dst, send_sem=q_ss.at[dx * SIDE + dy], recv_sem=q_rs.at[mine],
                    device_id=place(tx, ty, z), device_id_type=MESH)
                copy.start()
                q_sends.append(copy)

    def z_copy(xk, zk, step, ss):
        return pltpu.make_async_remote_copy(
            src_ref=kv.at[xk, :, :, zk], dst_ref=kv.at[xk, :, :, zk], send_sem=ss.at[xk, zk], recv_sem=z_rs.at[xk, zk],
            device_id=place(x, y, (z + step + SIDE) % SIDE), device_id_type=MESH)

    def send_up(xk, zk):
        @pl.when(z < SIDE - 1)
        def _():
            z_copy(xk, zk, 1, up_ss).start()

    def send_down(xk, zk):
        @pl.when(z > 0)
        def _():
            z_copy(xk, zk, -1, dn_ss).start()

    for xk in range(SIDE):
        for hk in range(2):
            for t in range(2):
                pltpu.make_async_copy(kv.at[xk, t, hk, z], kv.at[xk, t, hk, z], p_rs.at[t, xk, hk]).wait()
        send_up(xk, z)
        send_down(xk, z)

    def limits(i, carry):
        pos = (i * SIDE + z) * rows + lax.broadcasted_iota(jnp.int32, (rows, HEAD_DIM), 0)
        slot = pos // IMG * IMG
        found = jnp.zeros((rows, HEAD_DIM), jnp.int32)
        for n in range(maximg):
            first = jnp.where(n < count_ref[0], starts_ref[0, n], -1)
            found = jnp.where(slot == first, 1, found)
        lim[i] = jnp.where(found > 0, slot + (IMG - 1), pos)
        return carry

    lax.fori_loop(0, PLANE, limits, 0)

    def arrived(xk, zk):
        z_copy(xk, zk, 0, up_ss).wait_recv()

    @pl.when(inner > 0)
    def _():
        for d in range(1, SIDE):
            for xk in range(SIDE):
                @pl.when(z - d >= 0)
                def _():
                    arrived(xk, z - d)
                    send_up(xk, z - d)

                @pl.when(z + d <= SIDE - 1)
                def _():
                    arrived(xk, z + d)
                    send_down(xk, z + d)

    for i in range(PLANE):
        pltpu.make_async_copy(qg.at[i], qg.at[i], q_rs.at[i]).wait()

    keys = 2 * SIDE * rows
    y_low = half
    y_high = SIDE - 1 - half

    def tile(i, xk, masked):
        qq = qg[i]
        q = jnp.concatenate([qq[:, :HEAD_DIM], qq[:, HEAD_DIM:]], axis=0)
        k = kv[xk, 0].reshape(keys, HEAD_DIM)
        v = kv[xk, 1].reshape(keys, HEAD_DIM)
        s = lax.dot_general(q, k, (((1,), (1,)), ((), ())), preferred_element_type=jnp.float32)
        if masked:
            at = lax.broadcasted_iota(jnp.int32, (1, keys), 1)
            kpos = (xk * PLANE * rows) + at + jnp.where(at < keys // 2, y_low, y_high - 1) * (keys // 2)
            row_lim = lim[i]
            row_lim = jnp.concatenate([row_lim, row_lim], axis=0)[:, :1]
            seen = kpos <= row_lim
            s = jnp.where(seen, s, NEG)
        top = jnp.max(s, axis=1, keepdims=True)
        if xk > 0:
            before = mx[i][:, :1]
            top = jnp.maximum(top, before)
            shrink = jnp.exp2((before - top) * EXP2_SCALE)
        p = jnp.exp2((s - top) * EXP2_SCALE)
        if masked and xk == 0:
            p = jnp.where(seen, p, 0.0)
        total = jnp.sum(p, axis=1, keepdims=True)
        o = jnp.dot(p.astype(jnp.bfloat16), v, preferred_element_type=jnp.float32)
        if xk > 0:
            total = total + sm[i][:, :1] * shrink
            o = o + acc[i] * shrink
        if not masked:
            mx[i] = jnp.broadcast_to(top, (GROUP * rows, HEAD_DIM))
            sm[i] = jnp.broadcast_to(total, (GROUP * rows, HEAD_DIM))
            acc[i] = o
        else:
            o = (o / jnp.maximum(total, 1e-30)).astype(jnp.bfloat16)
            osend[i] = jnp.concatenate([o[:rows], o[rows:]], axis=1)
            lane = lax.broadcasted_iota(jnp.int32, (rows, HEAD_DIM), 1)
            stats = jnp.where(lane == 0, top[:rows], jnp.where(lane == 1, total[:rows], jnp.where(
                lane == 2, top[rows:], total[rows:])))
            stats = jnp.concatenate([stats, jnp.zeros((HEAD_DIM - rows, HEAD_DIM), jnp.float32)], axis=0)
            ssend[i] = stats.T[:8]

    def out_copies(xq, dy):
        ty = (y + dy) % SIDE
        i = xq * SIDE + ty
        to = place(xq, ty, z)
        a = pltpu.make_async_remote_copy(src_ref=osend.at[i], dst_ref=orecv.at[mine], send_sem=o_ss.at[xq, dy],
                                         recv_sem=o_rs.at[mine], device_id=to, device_id_type=MESH)
        b = pltpu.make_async_remote_copy(src_ref=ssend.at[i], dst_ref=srecv.at[mine], send_sem=s_ss.at[xq, dy],
                                         recv_sem=s_rs.at[mine], device_id=to, device_id_type=MESH)
        return a, b

    for xk in range(SIDE):
        @pl.when(z == 0)
        def _():
            for d in range(1, SIDE):
                arrived(xk, d)

        @pl.when(z == SIDE - 1)
        def _():
            for d in range(1, SIDE):
                arrived(xk, SIDE - 1 - d)

        def last(n, carry):
            tile(xk * SIDE + n, xk, True)
            return carry

        def more(n, carry):
            tile(n, xk, False)
            return carry

        lax.fori_loop(0, SIDE, last, 0)
        for dy in range(SIDE):
            own = (xk == x) if dy == 0 else None
            if dy == 0:
                @pl.when(x == xk)
                def _():
                    pltpu.make_async_copy(osend.at[mine], orecv.at[mine], o_rs.at[mine]).start()
                    pltpu.make_async_copy(ssend.at[mine], srecv.at[mine], s_rs.at[mine]).start()

                @pl.when(x != xk)
                def _():
                    for copy in out_copies(xk, 0):
                        copy.start()
            else:
                for copy in out_copies(xk, dy):
                    copy.start()
        if xk < SIDE - 1:
            lax.fori_loop(SIDE * (xk + 1), PLANE, more, 0)

    for i in range(PLANE):
        pltpu.make_async_copy(srecv.at[i], srecv.at[i], s_rs.at[i]).wait()
    shares = ([], [])
    for h in range(KV_HEADS):
        n0, n1 = SIDE * (h // 2) + 3 * (h % 2), SIDE * (h // 2) + 1 + h % 2
        a, b = srecv[n0], srecv[n1]
        top = jnp.maximum(a, b)
        wa = pltpu.roll(a, 7, 0) * jnp.exp2((a - top) * EXP2_SCALE)
        wb = pltpu.roll(b, 7, 0) * jnp.exp2((b - top) * EXP2_SCALE)
        row = lax.broadcasted_iota(jnp.int32, (8, HEAD_DIM), 0)
        good = (row == 0) | (row == 2)
        wa = jnp.where(good, wa, 1.0)
        wb = jnp.where(good, wb, 1.0)
        both = jnp.maximum(wa + wb, 1e-30)
        shares[0].append(wa / both)
        shares[1].append(wb / both)
    share = jnp.concatenate(shares[0] + shares[1], axis=0).T
    for h in range(KV_HEADS):
        n0, n1 = SIDE * (h // 2) + 3 * (h % 2), SIDE * (h // 2) + 1 + h % 2
        for n in (n0, n1):
            pltpu.make_async_copy(orecv.at[n], orecv.at[n], o_rs.at[n]).wait()
        a, b = orecv[n0].astype(jnp.float32), orecv[n1].astype(jnp.float32)
        for g in range(GROUP):
            part = pl.ds(h * WIDE + g * HEAD_DIM, HEAD_DIM)
            fa = share[:rows, 8 * h + 2 * g:8 * h + 2 * g + 1]
            fb = share[:rows, 64 + 8 * h + 2 * g:64 + 8 * h + 2 * g + 1]
            span = slice(g * HEAD_DIM, (g + 1) * HEAD_DIM)
            out_ref[:, part] = (a[:, span] * fa + b[:, span] * fb).astype(jnp.bfloat16)

    for copy in p_sends + q_sends:
        copy.wait_send()
    for xk in range(SIDE):
        for zk in range(SIDE):
            @pl.when((z < SIDE - 1) & (zk <= z))
            def _():
                z_copy(xk, zk, 1, up_ss).wait_send()

            @pl.when((z > 0) & (zk >= z))
            def _():
                z_copy(xk, zk, -1, dn_ss).wait_send()
        for dy in range(SIDE):
            @pl.when((x != xk) | (dy > 0))
            def _():
                for copy in out_copies(xk, dy):
                    copy.wait_send()


def shards(query_rows, key_rows, value_rows, image_starts, image_counts):
    rows = query_rows.shape[1]
    dma = pltpu.SemaphoreType.DMA
    vmem = pl.BlockSpec(memory_space=pltpu.VMEM)
    smem = pl.BlockSpec(memory_space=pltpu.SMEM)
    out = pl.pallas_call(
        kernel,
        out_shape=jax.ShapeDtypeStruct((rows, HEADS * HEAD_DIM), jnp.bfloat16),
        in_specs=[smem, smem, vmem, vmem, vmem],
        out_specs=vmem,
        scratch_shapes=[
            pltpu.VMEM((PLANE, rows, WIDE), jnp.bfloat16),
            pltpu.VMEM((SIDE, 2, 2, SIDE, rows, HEAD_DIM), jnp.bfloat16),
            pltpu.VMEM((PLANE, rows, HEAD_DIM), jnp.int32),
            pltpu.VMEM((PLANE, GROUP * rows, HEAD_DIM), jnp.float32),
            pltpu.VMEM((PLANE, GROUP * rows, HEAD_DIM), jnp.float32),
            pltpu.VMEM((PLANE, GROUP * rows, HEAD_DIM), jnp.float32),
            pltpu.VMEM((PLANE, rows, WIDE), jnp.bfloat16),
            pltpu.VMEM((PLANE, 8, HEAD_DIM), jnp.float32),
            pltpu.VMEM((PLANE, rows, WIDE), jnp.bfloat16),
            pltpu.VMEM((PLANE, 8, HEAD_DIM), jnp.float32),
            dma((PLANE,)), dma((PLANE,)),
            dma((16,)), dma((2, SIDE, 2)),
            dma((SIDE, SIDE)), dma((SIDE, SIDE)), dma((SIDE, SIDE)),
            dma((SIDE, SIDE)), dma((PLANE,)), dma((SIDE, SIDE)), dma((PLANE,)),
        ],
        compiler_params=pltpu.CompilerParams(collective_id=0, has_side_effects=True, vmem_limit_bytes=56 << 20),
        name="attend",
    )(image_starts, image_counts, query_rows[0], key_rows[0], value_rows[0])
    return out[None]


def solution(mesh):
    return jax.shard_map(
        shards,
        mesh=mesh,
        in_specs=(P("req", "ctx", None), P("req", "ctx", None), P("req", "ctx", None), P("req", None), P("req")),
        out_specs=P("req", "ctx", None),
        check_vma=False,
    )
```

```python
import math

import jax
import jax.numpy as jnp
from jax import lax
from jax.experimental import pallas as pl
from jax.experimental.pallas import tpu as pltpu
from jax.sharding import PartitionSpec as P

HEADS = 16
KV_HEADS = 8
HEAD_DIM = 128
IMG = 256
SIDE = 4
PLANE = SIDE * SIDE
GROUP = HEADS // KV_HEADS
WIDE = GROUP * HEAD_DIM
BLOCKS = 2 * SIDE
NEG = -1e30
MESH = pl.DeviceIdType.MESH

score_scale = 168.0 ** (-0.5)
EXP2_SCALE = score_scale * math.log2(math.e)

OWN_RIGHT, OWN_LEFT, FAR_RIGHT, FAR_LEFT, PASS_RIGHT, PASS_LEFT = range(6)


def kernel(starts_ref, count_ref, q_ref, k_ref, v_ref, out_ref,
           qg, kv, lim, acc, mx, osend,
           p_ss, p_rs, q_ss, q_rs, c_ss, c_rs, r_ss, r_rs, o_ss, o_rs):
    rows = q_ref.shape[0]
    maximg = starts_ref.shape[1]
    c = lax.axis_index("ctx")
    swap = lax.axis_index("req") % 2
    x, y, z = c // PLANE, (c // SIDE) % SIDE, c % SIDE
    a = x + swap * (y - x)
    s = y + swap * (x - y)
    near = 2 * (z // 2)
    far = 2 - near
    zi = z % 2
    pair = z + 1 - 2 * zi
    outer = (z + z // 2 + 1) % 2
    head = SIDE * outer + a
    is_self = (swap == 0) | (y % 2 == 0)

    def origin(xk):
        return y + swap * ((x - y - xk + 2 * SIDE) % SIDE - y)

    def chip(xx, yy, zz):
        return {"ctx": xx * PLANE + yy * SIDE + zz}

    def beside(step):
        ss = (s + step + SIDE) % SIDE
        return chip(a + swap * (ss - a), ss + swap * (a - ss), z)

    def keeper(aa, zz):
        return chip(aa + swap * ((x + y + aa) % SIDE - aa), y + swap * (aa - y), zz)

    left, right = beside(-1), beside(1)
    mirror = chip(x, y, SIDE - 1 - z)

    barrier = pltpu.get_barrier_semaphore()

    def hello(to):
        pl.semaphore_signal(barrier, inc=1, device_id=to, device_id_type=MESH)

    for d in range(SIDE):
        for zz in (z, pair):
            if d == 0 and zz is z:
                @pl.when(jnp.logical_not(is_self))
                def _():
                    hello(keeper(a, z))
                    hello(chip(x, origin(x), z))
            else:
                hello(keeper((a + d) % SIDE, zz))
                xx = (x + d) % SIDE
                hello(chip(xx, origin(xx), zz))
    for to in (left, right, mirror):
        hello(to)
    pl.semaphore_wait(barrier, 4 * SIDE + 3 - 2 * is_self.astype(jnp.int32))

    def cols(n, width):
        return pl.ds(pl.multiple_of(n * width, width), width)

    def first_copies(d, m, t):
        ta = (a + d) % SIDE
        th = SIDE * ((outer + m) % 2) + ta
        to = keeper(ta, pair if m else z)
        n = (d * 2 + m)
        if t < 2:
            src = (k_ref, v_ref)[t].at[:, cols(th, HEAD_DIM)]
            return src, kv.at[x, t, y, z], p_ss.at[t, n], p_rs.at[t, x, zi], to
        return q_ref.at[:, cols(th, WIDE)], qg.at[2 * x + zi], q_ss.at[n], q_rs.at[2 * x + zi], to

    def remote(src, dst, ss, rs, to):
        return pltpu.make_async_remote_copy(src_ref=src, dst_ref=dst, send_sem=ss, recv_sem=rs, device_id=to,
                                            device_id_type=MESH)

    def first(op, ts):
        for d in range(SIDE):
            for m in (1, 0):
                for t in ts:
                    src, dst, ss, rs, to = first_copies(d, m, t)
                    if d == 0 and m == 0:
                        if op == "start":
                            @pl.when(is_self)
                            def _():
                                pltpu.make_async_copy(src, dst, rs).start()

                        @pl.when(jnp.logical_not(is_self))
                        def _():
                            copy = remote(src, dst, ss, rs, to)
                            copy.start() if op == "start" else copy.wait_send()
                    else:
                        copy = remote(src, dst, ss, rs, to)
                        copy.start() if op == "start" else copy.wait_send()

    first("start", (0, 1))
    first("start", (2,))
    def limits(i, carry):
        pos = ((i // 2) * PLANE + origin(i // 2) * SIDE + near + i % 2) * rows + lax.broadcasted_iota(jnp.int32, (rows, HEAD_DIM), 0)
        slot = pos // IMG * IMG
        found = jnp.zeros((rows, HEAD_DIM), jnp.int32)
        for n in range(maximg):
            begin = jnp.where(n < count_ref[0], starts_ref[0, n], -1)
            found = jnp.where(slot == begin, 1, found)
        lim[i] = jnp.where(found > 0, slot + (IMG - 1), pos)
        mx[i] = jnp.full((GROUP * rows, HEAD_DIM), NEG, jnp.float32)
        acc[i] = jnp.zeros((GROUP * rows, WIDE), jnp.float32)
        return carry

    lax.fori_loop(0, BLOCKS, limits, 0)


    def part(xk, off, half):
        return kv.at[xk, :, (origin(xk) + off + SIDE) % SIDE, pl.ds(half, 2)]

    def cross(xk):
        return remote(part(xk, 0, near), part(xk, 0, near), c_ss.at[xk], c_rs.at[xk], mirror)

    def crossed(xk):
        remote(part(xk, 0, far), part(xk, 0, far), c_ss.at[xk], c_rs.at[xk], mirror).wait_recv()

    sent = {OWN_RIGHT: (0, near, right), OWN_LEFT: (0, near, left), FAR_RIGHT: (0, far, right),
            FAR_LEFT: (0, far, left), PASS_RIGHT: (-1, near, right), PASS_LEFT: (1, far, left)}
    shift = {OWN_RIGHT: -1, OWN_LEFT: 1, FAR_RIGHT: -1, FAR_LEFT: 1, PASS_RIGHT: -1, PASS_LEFT: 1}

    def ring(kind, xk):
        off, half, to = sent[kind]
        ref = part(xk, off, half)
        return remote(ref, ref, r_ss.at[kind, xk], r_rs.at[kind, xk], to)

    def ring_got(kind, xk):
        off, half, to = sent[kind]
        ref = part(xk, off + shift[kind], half)
        remote(ref, ref, r_ss.at[kind, xk], r_rs.at[kind, xk], to).wait_recv()

    for xk in range(SIDE):
        for t in range(2):
            for zz in range(2):
                ref = kv.at[xk, t, origin(xk), near + zz]
                pltpu.make_async_copy(ref, ref, p_rs.at[t, xk, zz]).wait()
        cross(xk).start()
        ring(OWN_RIGHT, xk).start()
        ring(OWN_LEFT, xk).start()

    def pass_own(xk):
        ring_got(OWN_RIGHT, xk)
        ring(PASS_RIGHT, xk).start()

    def send_far(xk):
        crossed(xk)
        ring(FAR_RIGHT, xk).start()
        ring(FAR_LEFT, xk).start()

    def pass_far(xk):
        ring_got(FAR_LEFT, xk)
        ring(PASS_LEFT, xk).start()

    def ready(xk):
        for kind in (OWN_LEFT, FAR_RIGHT, PASS_RIGHT, PASS_LEFT):
            ring_got(kind, xk)

    for xk in range(SIDE):
        pass_own(xk)
    keys = PLANE * rows

    def tile(xk, xq, masked):
        k = kv[xk, 0].reshape(keys, HEAD_DIM)
        v = jnp.concatenate([kv[xk, 1].reshape(keys, HEAD_DIM), jnp.ones((keys, HEAD_DIM), jnp.bfloat16)], axis=1)

        def scores(j):
            q = qg[2 * xq + j]
            q = jnp.concatenate([q[:, :HEAD_DIM], q[:, HEAD_DIM:]], axis=0)
            return lax.dot_general(q, k, (((1,), (1,)), ((), ())), preferred_element_type=jnp.float32)

        def weights(j, sc):
            if masked:
                at = lax.broadcasted_iota(jnp.int32, (1, keys), 1) + xk * keys
                row_lim = lim[2 * xq + j]
                sc = jnp.where(at <= jnp.concatenate([row_lim, row_lim], axis=0)[:, :1], sc, NEG)
            before = mx[2 * xq + j][:, :1]
            top = jnp.maximum(jnp.max(sc, axis=1, keepdims=True), before)
            mx[2 * xq + j] = jnp.broadcast_to(top, (GROUP * rows, HEAD_DIM))
            return jnp.exp2((sc - top) * EXP2_SCALE).astype(jnp.bfloat16), jnp.exp2((before - top) * EXP2_SCALE)

        def add(j, p, shrink):
            total = acc[2 * xq + j] * shrink + jnp.dot(p, v, preferred_element_type=jnp.float32)
            if not masked:
                acc[2 * xq + j] = total
            else:
                o = (total[:, :HEAD_DIM] / total[:, HEAD_DIM:]).astype(jnp.bfloat16)
                osend[2 * xq + j] = jnp.concatenate([o[:rows], o[rows:]], axis=1)

        s0 = scores(0)
        s1 = scores(1)
        p0 = weights(0, s0)
        p1 = weights(1, s1)
        add(0, *p0)
        add(1, *p1)

    def out_copy(op, xq):
        for j in range(2):
            src, dst = osend.at[2 * xq + j], out_ref.at[:, cols(head, WIDE)]
            here = (xq == x) & (origin(xq) == y) & (zi == j)
            if op == "start":
                @pl.when(here)
                def _():
                    pltpu.make_async_copy(src, dst, o_rs.at[head]).start()

            @pl.when(jnp.logical_not(here))
            def _():
                copy = remote(src, dst, o_ss.at[2 * xq + j], o_rs.at[head], chip(xq, origin(xq), near + j))
                copy.start() if op == "start" else copy.wait_send()

    def step(n, carry):
        xk = (n >= 4).astype(jnp.int32) + (n >= 7).astype(jnp.int32) + (n >= 9).astype(jnp.int32)
        xq = n - (4 * xk - xk * (xk - 1) // 2) + xk

        @pl.when(n == 0)
        def _():
            send_far(0)
            send_far(1)
            pass_far(0)
            for i in range(BLOCKS):
                pltpu.make_async_copy(qg.at[i], qg.at[i], q_rs.at[i]).wait()
            ready(0)

        @pl.when(n == 2)
        def _():
            send_far(2)
            pass_far(1)

        @pl.when(n == 4)
        def _():
            ready(1)

        @pl.when(n == 5)
        def _():
            send_far(3)
            pass_far(2)

        @pl.when(n == 6)
        def _():
            pass_far(3)

        @pl.when(n == 7)
        def _():
            ready(2)

        @pl.when(n == 9)
        def _():
            ready(3)

        @pl.when(xq == xk)
        def _():
            tile(xk, xq, True)
            out_copy("start", xq)

        @pl.when(xq != xk)
        def _():
            tile(xk, xq, False)
        return carry

    lax.fori_loop(0, SIDE * (SIDE + 1) // 2, step, 0)

    for h in range(KV_HEADS):
        ref = out_ref.at[:, pl.ds(h * WIDE, WIDE)]
        pltpu.make_async_copy(ref, ref, o_rs.at[h]).wait()
    first("wait", (0, 1, 2))
    for xk in range(SIDE):
        cross(xk).wait_send()
        for kind in range(6):
            ring(kind, xk).wait_send()
        out_copy("wait", xk)


def shards(query_rows, key_rows, value_rows, image_starts, image_counts):
    rows = query_rows.shape[1]
    dma = pltpu.SemaphoreType.DMA
    vmem = pl.BlockSpec(memory_space=pltpu.VMEM)
    smem = pl.BlockSpec(memory_space=pltpu.SMEM)
    out = pl.pallas_call(
        kernel,
        out_shape=jax.ShapeDtypeStruct((rows, HEADS * HEAD_DIM), jnp.bfloat16),
        in_specs=[smem, smem, vmem, vmem, vmem],
        out_specs=vmem,
        scratch_shapes=[
            pltpu.VMEM((BLOCKS, rows, WIDE), jnp.bfloat16),
            pltpu.VMEM((SIDE, 2, SIDE, SIDE, rows, HEAD_DIM), jnp.bfloat16),
            pltpu.VMEM((BLOCKS, rows, HEAD_DIM), jnp.int32),
            pltpu.VMEM((BLOCKS, GROUP * rows, WIDE), jnp.float32),
            pltpu.VMEM((BLOCKS, GROUP * rows, HEAD_DIM), jnp.float32),
            pltpu.VMEM((BLOCKS, rows, WIDE), jnp.bfloat16),
            dma((2, BLOCKS)), dma((2, SIDE, 2)), dma((BLOCKS,)), dma((BLOCKS,)),
            dma((SIDE,)), dma((SIDE,)), dma((6, SIDE)), dma((6, SIDE)), dma((BLOCKS,)), dma((KV_HEADS,)),
        ],
        compiler_params=pltpu.CompilerParams(collective_id=0, has_side_effects=True, vmem_limit_bytes=56 << 20),
        name="attend",
    )(image_starts, image_counts, query_rows[0], key_rows[0], value_rows[0])
    return out[None]


def solution(mesh):
    return jax.shard_map(
        shards,
        mesh=mesh,
        in_specs=(P("req", "ctx", None), P("req", "ctx", None), P("req", "ctx", None), P("req", None), P("req")),
        out_specs=P("req", "ctx", None),
        check_vma=False,
    )
```

```python
import math

import jax
import jax.numpy as jnp
from jax import lax
from jax.experimental import pallas as pl
from jax.experimental.pallas import tpu as pltpu
from jax.sharding import PartitionSpec as P

HEADS = 16
KV_HEADS = 8
HEAD_DIM = 128
IMG = 256
SIDE = 4
PLANE = SIDE * SIDE
GROUP = HEADS // KV_HEADS
WIDE = GROUP * HEAD_DIM
BLOCKS = 2 * SIDE
NEG = -1e30
MESH = pl.DeviceIdType.MESH

score_scale = 168.0 ** (-0.5)
EXP2_SCALE = score_scale * math.log2(math.e)


def kernel(starts_ref, count_ref, q_ref, k_ref, v_ref, out_ref,
           qg, kv, lim, acc, mx, osend,
           p_ss, p_rs, q_ss, q_rs, c_ss, c_rs, r_ss, r_rs, o_ss, o_rs):
    rows = q_ref.shape[0]
    maximg = starts_ref.shape[1]
    c = lax.axis_index("ctx")
    swap = lax.axis_index("req") % 2
    x, y, z = c // PLANE, (c // SIDE) % SIDE, c % SIDE
    a = x + swap * (y - x)
    s = y + swap * (x - y)
    near = 2 * (z // 2)
    far = 2 - near
    zi = z % 2
    pair = z + 1 - 2 * zi
    outer = (z + z // 2 + 1) % 2
    head = SIDE * outer + a
    is_self = (swap == 0) | (y % 2 == 0)

    def origin(xk):
        return y + swap * ((x - y - xk + 2 * SIDE) % SIDE - y)

    def chip(xx, yy, zz):
        return {"ctx": xx * PLANE + yy * SIDE + zz}

    def beside(step):
        ss = (s + step + SIDE) % SIDE
        return chip(a + swap * (ss - a), ss + swap * (a - ss), z)

    def keeper(aa, zz):
        return chip(aa + swap * ((x + y + aa) % SIDE - aa), y + swap * (aa - y), zz)

    mirror = chip(x, y, SIDE - 1 - z)

    barrier = pltpu.get_barrier_semaphore()

    def hello(to):
        pl.semaphore_signal(barrier, inc=1, device_id=to, device_id_type=MESH)

    for d in range(SIDE):
        for zz in (z, pair):
            if d == 0 and zz is z:
                @pl.when(jnp.logical_not(is_self))
                def _():
                    hello(keeper(a, z))
                    hello(chip(x, origin(x), z))
            else:
                hello(keeper((a + d) % SIDE, zz))
                xx = (x + d) % SIDE
                hello(chip(xx, origin(xx), zz))
    for step in range(1, SIDE):
        hello(beside(step))
    hello(mirror)
    pl.semaphore_wait(barrier, 5 * SIDE - 2 * is_self.astype(jnp.int32))

    def cols(n, width):
        return pl.ds(pl.multiple_of(n * width, width), width)

    def first_copies(d, m, t):
        ta = (a + d) % SIDE
        th = SIDE * ((outer + m) % 2) + ta
        to = keeper(ta, pair if m else z)
        n = (d * 2 + m)
        if t < 2:
            src = (k_ref, v_ref)[t].at[:, cols(th, HEAD_DIM)]
            return src, kv.at[x, t, y, z], p_ss.at[t, n], p_rs.at[t, x, zi], to
        return q_ref.at[:, cols(th, WIDE)], qg.at[2 * x + zi], q_ss.at[n], q_rs.at[2 * x + zi], to

    def remote(src, dst, ss, rs, to):
        return pltpu.make_async_remote_copy(src_ref=src, dst_ref=dst, send_sem=ss, recv_sem=rs, device_id=to,
                                            device_id_type=MESH)

    def first(op, ts):
        for d in (0, 3, 1, 2):
            for m in (1, 0):
                for t in ts:
                    src, dst, ss, rs, to = first_copies(d, m, t)
                    if d == 0 and m == 0:
                        if op == "start":
                            @pl.when(is_self)
                            def _():
                                pltpu.make_async_copy(src, dst, rs).start()

                        @pl.when(jnp.logical_not(is_self))
                        def _():
                            copy = remote(src, dst, ss, rs, to)
                            copy.start() if op == "start" else copy.wait_send()
                    else:
                        copy = remote(src, dst, ss, rs, to)
                        copy.start() if op == "start" else copy.wait_send()

    first("start", (0, 1))
    first("start", (2,))
    def limits(i, carry):
        pos = ((i // 2) * PLANE + origin(i // 2) * SIDE + near + i % 2) * rows + lax.broadcasted_iota(jnp.int32, (rows, HEAD_DIM), 0)
        slot = pos // IMG * IMG
        found = jnp.zeros((rows, HEAD_DIM), jnp.int32)
        for n in range(maximg):
            begin = jnp.where(n < count_ref[0], starts_ref[0, n], -1)
            found = jnp.where(slot == begin, 1, found)
        lim[i] = jnp.where(found > 0, slot + (IMG - 1), pos)
        mx[i] = jnp.full((GROUP * rows, HEAD_DIM), NEG, jnp.float32)
        acc[i] = jnp.zeros((GROUP * rows, WIDE), jnp.float32)
        return carry

    lax.fori_loop(0, BLOCKS, limits, 0)


    def part(xk, off, half):
        return kv.at[xk, :, (origin(xk) + off + SIDE) % SIDE, pl.ds(half, 2)]

    def cross(xk):
        return remote(part(xk, 0, near), part(xk, 0, near), c_ss.at[xk], c_rs.at[xk], mirror)

    def crossed(xk):
        remote(part(xk, 0, far), part(xk, 0, far), c_ss.at[xk], c_rs.at[xk], mirror).wait_recv()

    def ring(xk, side, step):
        ref = part(xk, 0, far if side else near)
        n = (xk * 2 + side) * SIDE + step
        return remote(ref, ref, r_ss.at[n], r_rs.at[n], beside(step))

    def ring_got(xk, side, step):
        ref = part(xk, SIDE - step, far if side else near)
        n = (xk * 2 + side) * SIDE + step
        remote(ref, ref, r_ss.at[n], r_rs.at[n], beside(step)).wait_recv()

    def send_near(xk):
        for turn in (1, 3, 2):
            ring(xk, 0, turn).start()

    soon = x + swap * ((x - 2 * y + 2 * SIDE) % SIDE - x)

    def order(i):
        return soon if i == 0 else i - 1 + (soon <= i - 1).astype(jnp.int32)

    for i in range(SIDE):
        xk = order(i)
        for t in range(2):
            for zz in range(2):
                ref = kv.at[xk, t, origin(xk), near + zz]
                pltpu.make_async_copy(ref, ref, p_rs.at[t, xk, zz]).wait()
        cross(xk).start()
        if i < 4:
            send_near(xk)

    def send_far(xk):
        crossed(xk)
        for turn in (1, 3, 2):
            ring(xk, 1, turn).start()

    def ready(xk):
        for turn in range(1, SIDE):
            for side in range(2):
                ring_got(xk, side, turn)

    keys = PLANE * rows

    def out_copy(op, xq, j):
        src, dst = osend.at[2 * xq + j], out_ref.at[:, cols(head, WIDE)]
        here = (xq == x) & (origin(xq) == y) & (zi == j)
        if op == "start":
            @pl.when(here)
            def _():
                pltpu.make_async_copy(src, dst, o_rs.at[head]).start()

        @pl.when(jnp.logical_not(here))
        def _():
            copy = remote(src, dst, o_ss.at[2 * xq + j], o_rs.at[head], chip(xq, origin(xq), near + j))
            copy.start() if op == "start" else copy.wait_send()

    def tile(xk, xq, masked):
        k = kv[xk, 0].reshape(keys, HEAD_DIM)
        v = jnp.concatenate([kv[xk, 1].reshape(keys, HEAD_DIM), jnp.ones((keys, HEAD_DIM), jnp.bfloat16)], axis=1)

        def scores(j):
            q = qg[2 * xq + j]
            q = jnp.concatenate([q[:, :HEAD_DIM], q[:, HEAD_DIM:]], axis=0)
            return lax.dot_general(q, k, (((1,), (1,)), ((), ())), preferred_element_type=jnp.float32)

        def weights(j, sc):
            if masked:
                at = lax.broadcasted_iota(jnp.int32, (1, keys), 1) + xk * keys
                row_lim = lim[2 * xq + j]
                sc = jnp.where(at <= jnp.concatenate([row_lim, row_lim], axis=0)[:, :1], sc, NEG)
            before = mx[2 * xq + j][:, :1]
            top = jnp.maximum(jnp.max(sc, axis=1, keepdims=True), before)
            mx[2 * xq + j] = jnp.broadcast_to(top, (GROUP * rows, HEAD_DIM))
            return jnp.exp2((sc - top) * EXP2_SCALE).astype(jnp.bfloat16), jnp.exp2((before - top) * EXP2_SCALE)

        def add(j, p, shrink):
            total = acc[2 * xq + j] * shrink + jnp.dot(p, v, preferred_element_type=jnp.float32)
            if not masked:
                acc[2 * xq + j] = total
            else:
                o = (total[:, :HEAD_DIM] / total[:, HEAD_DIM:]).astype(jnp.bfloat16)
                osend[2 * xq + j] = jnp.concatenate([o[:rows], o[rows:]], axis=1)

        s0 = scores(0)
        s1 = scores(1)
        p0 = weights(0, s0)
        if masked:
            add(0, *p0)
            out_copy("start", xq, 0)
            add(1, *weights(1, s1))
            out_copy("start", xq, 1)
        else:
            p1 = weights(1, s1)
            add(0, *p0)
            add(1, *p1)

    def step(n, carry):
        xk = (n >= 4).astype(jnp.int32) + (n >= 7).astype(jnp.int32) + (n >= 9).astype(jnp.int32)
        xq = n - (4 * xk - xk * (xk - 1) // 2) + xk

        @pl.when(n == 0)
        def _():
            send_far(order(0))
            send_far(order(1))
            for i in range(BLOCKS):
                pltpu.make_async_copy(qg.at[i], qg.at[i], q_rs.at[i]).wait()
            ready(0)

        @pl.when(n == 1)
        def _():
            send_far(order(2))

        @pl.when(n == 4)
        def _():
            ready(1)
            send_far(order(3))

        @pl.when(n == 7)
        def _():
            ready(2)

        @pl.when(n == 9)
        def _():
            ready(3)

        @pl.when(xq == xk)
        def _():
            tile(xk, xq, True)

        @pl.when(xq != xk)
        def _():
            tile(xk, xq, False)
        return carry

    lax.fori_loop(0, SIDE * (SIDE + 1) // 2, step, 0)

    for h in range(KV_HEADS):
        ref = out_ref.at[:, pl.ds(h * WIDE, WIDE)]
        pltpu.make_async_copy(ref, ref, o_rs.at[h]).wait()
    first("wait", (0, 1, 2))
    for xk in range(SIDE):
        cross(xk).wait_send()
        for side in range(2):
            for turn in range(1, SIDE):
                ring(xk, side, turn).wait_send()
        for j in range(2):
            out_copy("wait", xk, j)


def shards(query_rows, key_rows, value_rows, image_starts, image_counts):
    rows = query_rows.shape[1]
    dma = pltpu.SemaphoreType.DMA
    smem = pl.BlockSpec(memory_space=pltpu.SMEM)
    hbm = pl.BlockSpec(memory_space=pltpu.HBM)
    out = pl.pallas_call(
        kernel,
        out_shape=jax.ShapeDtypeStruct((rows, HEADS * HEAD_DIM), jnp.bfloat16),
        in_specs=[smem, smem, hbm, hbm, hbm],
        out_specs=hbm,
        scratch_shapes=[
            pltpu.VMEM((BLOCKS, rows, WIDE), jnp.bfloat16),
            pltpu.VMEM((SIDE, 2, SIDE, SIDE, rows, HEAD_DIM), jnp.bfloat16),
            pltpu.VMEM((BLOCKS, rows, HEAD_DIM), jnp.int32),
            pltpu.VMEM((BLOCKS, GROUP * rows, WIDE), jnp.float32),
            pltpu.VMEM((BLOCKS, GROUP * rows, HEAD_DIM), jnp.float32),
            pltpu.VMEM((BLOCKS, rows, WIDE), jnp.bfloat16),
            dma((2, BLOCKS)), dma((2, SIDE, 2)), dma((BLOCKS,)), dma((BLOCKS,)),
            dma((SIDE,)), dma((SIDE,)), dma((2 * PLANE,)), dma((2 * PLANE,)), dma((BLOCKS,)), dma((KV_HEADS,)),
        ],
        compiler_params=pltpu.CompilerParams(collective_id=0, has_side_effects=True, vmem_limit_bytes=56 << 20),
        name="attend",
    )(image_starts, image_counts, query_rows[0], key_rows[0], value_rows[0])
    return out[None]


def solution(mesh):
    return jax.shard_map(
        shards,
        mesh=mesh,
        in_specs=(P("req", "ctx", None), P("req", "ctx", None), P("req", "ctx", None), P("req", None), P("req")),
        out_specs=P("req", "ctx", None),
        check_vma=False,
    )
```

```python
import math

import jax
import jax.numpy as jnp
from jax import lax
from jax.experimental import pallas as pl
from jax.experimental.pallas import tpu as pltpu
from jax.sharding import PartitionSpec as P

HEADS = 16
KV_HEADS = 8
HEAD_DIM = 128
IMG = 256
SIDE = 4
PLANE = SIDE * SIDE
GROUP = HEADS // KV_HEADS
WIDE = GROUP * HEAD_DIM
BLOCKS = 2 * SIDE
NEG = -1e30
MESH = pl.DeviceIdType.MESH

score_scale = 168.0 ** (-0.5)
EXP2_SCALE = score_scale * math.log2(math.e)


def kernel(starts_ref, count_ref, q_ref, k_ref, v_ref, out_ref,
           qg, kv, lim, acc, mx, osend,
           p_ss, p_rs, q_ss, q_rs, c_ss, c_rs, r_ss, r_rs, o_ss, o_rs):
    rows = q_ref.shape[0]
    maximg = starts_ref.shape[1]
    c = lax.axis_index("ctx")
    swap = lax.axis_index("req") % 2
    x, y, z = c // PLANE, (c // SIDE) % SIDE, c % SIDE
    a = x + swap * (y - x)
    s = y + swap * (x - y)
    near = 2 * (z // 2)
    far = 2 - near
    zi = z % 2
    pair = z + 1 - 2 * zi
    outer = (z + z // 2 + 1) % 2
    head = SIDE * outer + a
    is_self = (swap == 0) | (y % 2 == 0)

    def origin(xk):
        return y + swap * ((x - y - xk + 2 * SIDE) % SIDE - y)

    def chip(xx, yy, zz):
        return {"ctx": xx * PLANE + yy * SIDE + zz}

    def beside(step):
        ss = (s + step + SIDE) % SIDE
        return chip(a + swap * (ss - a), ss + swap * (a - ss), z)

    def keeper(aa, zz):
        return chip(aa + swap * ((x + y + aa) % SIDE - aa), y + swap * (aa - y), zz)

    mirror = chip(x, y, SIDE - 1 - z)

    barrier = pltpu.get_barrier_semaphore()

    def hello(to):
        pl.semaphore_signal(barrier, inc=1, device_id=to, device_id_type=MESH)

    for d in range(SIDE):
        for zz in (z, pair):
            if d == 0 and zz is z:
                @pl.when(jnp.logical_not(is_self))
                def _():
                    hello(keeper(a, z))
                    hello(chip(x, origin(x), z))
            else:
                hello(keeper((a + d) % SIDE, zz))
                xx = (x + d) % SIDE
                hello(chip(xx, origin(xx), zz))
    for step in range(1, SIDE):
        hello(beside(step))
    hello(mirror)
    pl.semaphore_wait(barrier, 5 * SIDE - 2 * is_self.astype(jnp.int32))

    def cols(n, width):
        return pl.ds(pl.multiple_of(n * width, width), width)

    def first_copies(d, m, t):
        ta = (a + d) % SIDE
        th = SIDE * ((outer + m) % 2) + ta
        to = keeper(ta, pair if m else z)
        n = (d * 2 + m)
        if t < 2:
            src = (k_ref, v_ref)[t].at[:, cols(th, HEAD_DIM)]
            return src, kv.at[x, t, y, z], p_ss.at[t, n], p_rs.at[t, x, zi], to
        return q_ref.at[:, cols(th, WIDE)], qg.at[2 * x + zi], q_ss.at[n], q_rs.at[2 * x + zi], to

    def remote(src, dst, ss, rs, to):
        return pltpu.make_async_remote_copy(src_ref=src, dst_ref=dst, send_sem=ss, recv_sem=rs, device_id=to,
                                            device_id_type=MESH)

    def first(op, ts):
        for d in (0, 3, 1, 2):
            for m in (1, 0):
                for t in ts:
                    src, dst, ss, rs, to = first_copies(d, m, t)
                    if d == 0 and m == 0:
                        if op == "start":
                            @pl.when(is_self)
                            def _():
                                pltpu.make_async_copy(src, dst, rs).start()

                        @pl.when(jnp.logical_not(is_self))
                        def _():
                            copy = remote(src, dst, ss, rs, to)
                            copy.start() if op == "start" else copy.wait_send()
                    else:
                        copy = remote(src, dst, ss, rs, to)
                        copy.start() if op == "start" else copy.wait_send()

    first("start", (0, 1))
    first("start", (2,))
    def limits(i, carry):
        pos = ((i // 2) * PLANE + origin(i // 2) * SIDE + near + i % 2) * rows + lax.broadcasted_iota(jnp.int32, (rows, HEAD_DIM), 0)
        slot = pos // IMG * IMG
        found = jnp.zeros((rows, HEAD_DIM), jnp.int32)
        for n in range(maximg):
            begin = jnp.where(n < count_ref[0], starts_ref[0, n], -1)
            found = jnp.where(slot == begin, 1, found)
        lim[i] = jnp.where(found > 0, slot + (IMG - 1), pos)
        mx[i] = jnp.full((GROUP * rows, HEAD_DIM), NEG, jnp.float32)
        acc[i] = jnp.zeros((GROUP * rows, WIDE), jnp.float32)
        return carry

    lax.fori_loop(0, BLOCKS, limits, 0)


    def part(xk, off, half):
        return kv.at[xk, :, (origin(xk) + off + SIDE) % SIDE, pl.ds(half, 2)]

    def cross(xk):
        return remote(part(xk, 0, near), part(xk, 0, near), c_ss.at[xk], c_rs.at[xk], mirror)

    def crossed(xk):
        remote(part(xk, 0, far), part(xk, 0, far), c_ss.at[xk], c_rs.at[xk], mirror).wait_recv()

    def ring(xk, side, step):
        ref = part(xk, 0, far if side else near)
        n = (xk * 2 + side) * SIDE + step
        return remote(ref, ref, r_ss.at[n], r_rs.at[n], beside(step))

    def ring_got(xk, side, step):
        ref = part(xk, SIDE - step, far if side else near)
        n = (xk * 2 + side) * SIDE + step
        remote(ref, ref, r_ss.at[n], r_rs.at[n], beside(step)).wait_recv()

    def send_near(xk):
        for turn in (1, 3, 2):
            ring(xk, 0, turn).start()

    soon = x + swap * ((x - 2 * y + 2 * SIDE) % SIDE - x)

    def order(i):
        return soon if i == 0 else i - 1 + (soon <= i - 1).astype(jnp.int32)

    for i in range(SIDE):
        xk = order(i)
        for t in range(2):
            for zz in range(2):
                ref = kv.at[xk, t, origin(xk), near + zz]
                pltpu.make_async_copy(ref, ref, p_rs.at[t, xk, zz]).wait()
        cross(xk).start()
        if i < 4:
            send_near(xk)

    def send_far(xk):
        crossed(xk)
        for turn in (1, 3, 2):
            ring(xk, 1, turn).start()

    def ready(xk):
        for turn in range(1, SIDE):
            for side in range(2):
                ring_got(xk, side, turn)

    keys = PLANE * rows

    def out_copy(op, xq, j):
        src, dst = osend.at[2 * xq + j], out_ref.at[:, cols(head, WIDE)]
        here = (xq == x) & (origin(xq) == y) & (zi == j)
        if op == "start":
            @pl.when(here)
            def _():
                pltpu.make_async_copy(src, dst, o_rs.at[head]).start()

        @pl.when(jnp.logical_not(here))
        def _():
            copy = remote(src, dst, o_ss.at[2 * xq + j], o_rs.at[head], chip(xq, origin(xq), near + j))
            copy.start() if op == "start" else copy.wait_send()

    def scores(xk, i):
        q = qg[i]
        q = jnp.concatenate([q[:, :HEAD_DIM], q[:, HEAD_DIM:]], axis=0)
        k = kv[xk, 0].reshape(keys, HEAD_DIM)
        return lax.dot_general(q, k, (((1,), (1,)), ((), ())), preferred_element_type=jnp.float32)

    def weights(xk, i, sc):
        if i // 2 == xk:
            at = lax.broadcasted_iota(jnp.int32, (1, keys), 1) + xk * keys
            row_lim = lim[i]
            sc = jnp.where(at <= jnp.concatenate([row_lim, row_lim], axis=0)[:, :1], sc, NEG)
        before = mx[i][:, :1]
        top = jnp.maximum(jnp.max(sc, axis=1, keepdims=True), before)
        mx[i] = jnp.broadcast_to(top, (GROUP * rows, HEAD_DIM))
        return jnp.exp2((sc - top) * EXP2_SCALE).astype(jnp.bfloat16), jnp.exp2((before - top) * EXP2_SCALE)

    def add(xk, i, p, shrink):
        v = jnp.concatenate([kv[xk, 1].reshape(keys, HEAD_DIM), jnp.ones((keys, HEAD_DIM), jnp.bfloat16)], axis=1)
        total = acc[i] * shrink + jnp.dot(p, v, preferred_element_type=jnp.float32)
        if i // 2 > xk:
            acc[i] = total
        else:
            o = (total[:, :HEAD_DIM] / total[:, HEAD_DIM:]).astype(jnp.bfloat16)
            osend[i] = jnp.concatenate([o[:rows], o[rows:]], axis=1)

    def run(units):
        sc, held = scores(*units[0]), None
        for n, unit in enumerate(units):
            later = scores(*units[n + 1]) if n + 1 < len(units) else None
            p = weights(*unit, sc)
            if held is not None:
                add(*held)
            held, sc = (*unit, *p), later
        add(*held)

    def plane(xk):
        run([(xk, i) for i in range(2 * xk, BLOCKS)])
        for j in range(2):
            out_copy("start", xk, j)

    for n in range(SIDE):
        send_far(order(n))
    for i in range(BLOCKS):
        pltpu.make_async_copy(qg.at[i], qg.at[i], q_rs.at[i]).wait()
    for xk in range(SIDE):
        ready(xk)
        plane(xk)

    for h in range(KV_HEADS):
        ref = out_ref.at[:, pl.ds(h * WIDE, WIDE)]
        pltpu.make_async_copy(ref, ref, o_rs.at[h]).wait()
    first("wait", (0, 1, 2))
    for xk in range(SIDE):
        cross(xk).wait_send()
        for side in range(2):
            for turn in range(1, SIDE):
                ring(xk, side, turn).wait_send()
        for j in range(2):
            out_copy("wait", xk, j)


def shards(query_rows, key_rows, value_rows, image_starts, image_counts):
    rows = query_rows.shape[1]
    dma = pltpu.SemaphoreType.DMA
    smem = pl.BlockSpec(memory_space=pltpu.SMEM)
    hbm = pl.BlockSpec(memory_space=pltpu.HBM)
    out = pl.pallas_call(
        kernel,
        out_shape=jax.ShapeDtypeStruct((rows, HEADS * HEAD_DIM), jnp.bfloat16),
        in_specs=[smem, smem, hbm, hbm, hbm],
        out_specs=hbm,
        scratch_shapes=[
            pltpu.VMEM((BLOCKS, rows, WIDE), jnp.bfloat16),
            pltpu.VMEM((SIDE, 2, SIDE, SIDE, rows, HEAD_DIM), jnp.bfloat16),
            pltpu.VMEM((BLOCKS, rows, HEAD_DIM), jnp.int32),
            pltpu.VMEM((BLOCKS, GROUP * rows, WIDE), jnp.float32),
            pltpu.VMEM((BLOCKS, GROUP * rows, HEAD_DIM), jnp.float32),
            pltpu.VMEM((BLOCKS, rows, WIDE), jnp.bfloat16),
            dma((2, BLOCKS)), dma((2, SIDE, 2)), dma((BLOCKS,)), dma((BLOCKS,)),
            dma((SIDE,)), dma((SIDE,)), dma((2 * PLANE,)), dma((2 * PLANE,)), dma((BLOCKS,)), dma((KV_HEADS,)),
        ],
        compiler_params=pltpu.CompilerParams(collective_id=0, has_side_effects=True, vmem_limit_bytes=56 << 20),
        name="attend",
    )(image_starts, image_counts, query_rows[0], key_rows[0], value_rows[0])
    return out[None]


def solution(mesh):
    return jax.shard_map(
        shards,
        mesh=mesh,
        in_specs=(P("req", "ctx", None), P("req", "ctx", None), P("req", "ctx", None), P("req", None), P("req")),
        out_specs=P("req", "ctx", None),
        check_vma=False,
    )
```

```python
import math

import jax
import jax.numpy as jnp
from jax import lax
from jax.experimental import pallas as pl
from jax.experimental.pallas import tpu as pltpu
from jax.sharding import PartitionSpec as P

HEADS = 16
KV_HEADS = 8
HEAD_DIM = 128
IMG = 256
SIDE = 4
PLANE = SIDE * SIDE
GROUP = HEADS // KV_HEADS
WIDE = GROUP * HEAD_DIM
BLOCKS = 2 * SIDE
NEG = -1e30
MESH = pl.DeviceIdType.MESH

score_scale = 168.0 ** (-0.5)
EXP2_SCALE = score_scale * math.log2(math.e)


def kernel(starts_ref, count_ref, q_ref, k_ref, v_ref, out_ref,
           qg, kv, lim, acc, mx, osend,
           p_ss, p_rs, q_ss, q_rs, c_ss, c_rs, r_ss, r_rs, o_ss, o_rs):
    rows = q_ref.shape[0]
    maximg = starts_ref.shape[1]
    c = lax.axis_index("ctx")
    swap = lax.axis_index("req") % 2
    x, y, z = c // PLANE, (c // SIDE) % SIDE, c % SIDE
    a = x + swap * (y - x)
    s = y + swap * (x - y)
    near = 2 * (z // 2)
    far = 2 - near
    zi = z % 2
    pair = z + 1 - 2 * zi
    outer = (z + z // 2 + 1) % 2
    head = SIDE * outer + a
    is_self = (swap == 0) | (y % 2 == 0)

    def origin(xk):
        return y + swap * ((x - y - xk + 2 * SIDE) % SIDE - y)

    def chip(xx, yy, zz):
        return {"ctx": xx * PLANE + yy * SIDE + zz}

    def beside(step):
        ss = (s + step + SIDE) % SIDE
        return chip(a + swap * (ss - a), ss + swap * (a - ss), z)

    def keeper(aa, zz):
        return chip(aa + swap * ((x + y + aa) % SIDE - aa), y + swap * (aa - y), zz)

    mirror = chip(x, y, SIDE - 1 - z)

    barrier = pltpu.get_barrier_semaphore()

    def hello(to):
        pl.semaphore_signal(barrier, inc=1, device_id=to, device_id_type=MESH)

    for d in range(SIDE):
        for zz in (z, pair):
            if d == 0 and zz is z:
                @pl.when(jnp.logical_not(is_self))
                def _():
                    hello(keeper(a, z))
                    hello(chip(x, origin(x), z))
            else:
                hello(keeper((a + d) % SIDE, zz))
                xx = (x + d) % SIDE
                hello(chip(xx, origin(xx), zz))
    for step in range(1, SIDE):
        hello(beside(step))
    hello(mirror)
    pl.semaphore_wait(barrier, 5 * SIDE - 2 * is_self.astype(jnp.int32))

    def cols(n, width):
        return pl.ds(pl.multiple_of(n * width, width), width)

    def first_copies(d, m, t):
        ta = (a + d) % SIDE
        th = SIDE * ((outer + m) % 2) + ta
        to = keeper(ta, pair if m else z)
        n = (d * 2 + m)
        if t < 2:
            src = (k_ref, v_ref)[t].at[:, cols(th, HEAD_DIM)]
            return src, kv.at[x, t, y, z], p_ss.at[t, n], p_rs.at[t, x, zi], to
        return q_ref.at[:, cols(th, WIDE)], qg.at[2 * x + zi], q_ss.at[n], q_rs.at[2 * x + zi], to

    def remote(src, dst, ss, rs, to):
        return pltpu.make_async_remote_copy(src_ref=src, dst_ref=dst, send_sem=ss, recv_sem=rs, device_id=to,
                                            device_id_type=MESH)

    def first(op, ts):
        for d in (0, 3, 1, 2):
            for m in (1, 0):
                for t in ts:
                    src, dst, ss, rs, to = first_copies(d, m, t)
                    if d == 0 and m == 0:
                        if op == "start":
                            @pl.when(is_self)
                            def _():
                                pltpu.make_async_copy(src, dst, rs).start()

                        @pl.when(jnp.logical_not(is_self))
                        def _():
                            copy = remote(src, dst, ss, rs, to)
                            copy.start() if op == "start" else copy.wait_send()
                    else:
                        copy = remote(src, dst, ss, rs, to)
                        copy.start() if op == "start" else copy.wait_send()

    first("start", (0, 1))
    first("start", (2,))
    def limits(i, carry):
        pos = ((i // 2) * PLANE + origin(i // 2) * SIDE + near + i % 2) * rows + lax.broadcasted_iota(jnp.int32, (rows, HEAD_DIM), 0)
        slot = pos // IMG * IMG
        found = jnp.zeros((rows, HEAD_DIM), jnp.int32)
        for n in range(maximg):
            begin = jnp.where(n < count_ref[0], starts_ref[0, n], -1)
            found = jnp.where(slot == begin, 1, found)
        lim[i] = jnp.where(found > 0, slot + (IMG - 1), pos)
        mx[i] = jnp.full((GROUP * rows, HEAD_DIM), NEG, jnp.float32)
        acc[i] = jnp.zeros((GROUP * rows, WIDE), jnp.float32)
        return carry

    lax.fori_loop(0, BLOCKS, limits, 0)


    def part(xk, off, half):
        return kv.at[xk, :, (origin(xk) + off + SIDE) % SIDE, pl.ds(half, 2)]

    def cross(xk):
        return remote(part(xk, 0, near), part(xk, 0, near), c_ss.at[xk], c_rs.at[xk], mirror)

    def crossed(xk):
        remote(part(xk, 0, far), part(xk, 0, far), c_ss.at[xk], c_rs.at[xk], mirror).wait_recv()

    def ring(xk, side, step):
        ref = part(xk, 0, far if side else near)
        n = (xk * 2 + side) * SIDE + step
        return remote(ref, ref, r_ss.at[n], r_rs.at[n], beside(step))

    def ring_got(xk, side, step):
        ref = part(xk, SIDE - step, far if side else near)
        n = (xk * 2 + side) * SIDE + step
        remote(ref, ref, r_ss.at[n], r_rs.at[n], beside(step)).wait_recv()

    def send_near(xk):
        for turn in (1, 3):
            ring(xk, 0, turn).start()

    soon = x + swap * ((x - 2 * y + 2 * SIDE) % SIDE - x)

    def order(i):
        return soon if i == 0 else i - 1 + (soon <= i - 1).astype(jnp.int32)

    for i in range(SIDE):
        xk = order(i)
        for t in range(2):
            for zz in range(2):
                ref = kv.at[xk, t, origin(xk), near + zz]
                pltpu.make_async_copy(ref, ref, p_rs.at[t, xk, zz]).wait()
        cross(xk).start()
        if i < 4:
            send_near(xk)

    def pass_on(xk):
        n = xk * 2 * SIDE + 2
        ref = part(xk, SIDE - 1, near)
        return remote(ref, ref, r_ss.at[n], r_rs.at[n], beside(1))

    for xk in range(SIDE):
        ring_got(xk, 0, 1)
        pass_on(xk).start()

    def send_far(xk):
        crossed(xk)
        for turn in (1, 3, 2):
            ring(xk, 1, turn).start()

    def ready(xk):
        for turn in range(1, SIDE):
            for side in range(2):
                if side or turn > 1:
                    ring_got(xk, side, turn)

    keys = PLANE * rows

    def out_copy(op, xq, j):
        src, dst = osend.at[2 * xq + j], out_ref.at[:, cols(head, WIDE)]
        here = (xq == x) & (origin(xq) == y) & (zi == j)
        if op == "start":
            @pl.when(here)
            def _():
                pltpu.make_async_copy(src, dst, o_rs.at[head]).start()

        @pl.when(jnp.logical_not(here))
        def _():
            copy = remote(src, dst, o_ss.at[2 * xq + j], o_rs.at[head], chip(xq, origin(xq), near + j))
            copy.start() if op == "start" else copy.wait_send()

    def scores(xk, i):
        q = qg[i]
        q = jnp.concatenate([q[:, :HEAD_DIM], q[:, HEAD_DIM:]], axis=0)
        k = kv[xk, 0].reshape(keys, HEAD_DIM)
        return lax.dot_general(q, k, (((1,), (1,)), ((), ())), preferred_element_type=jnp.float32)

    def weights(xk, i, sc):
        if i // 2 == xk:
            at = lax.broadcasted_iota(jnp.int32, (1, keys), 1) + xk * keys
            row_lim = lim[i]
            sc = jnp.where(at <= jnp.concatenate([row_lim, row_lim], axis=0)[:, :1], sc, NEG)
        before = mx[i][:, :1]
        top = jnp.maximum(jnp.max(sc, axis=1, keepdims=True), before)
        mx[i] = jnp.broadcast_to(top, (GROUP * rows, HEAD_DIM))
        return jnp.exp2((sc - top) * EXP2_SCALE).astype(jnp.bfloat16), jnp.exp2((before - top) * EXP2_SCALE)

    def add(xk, i, p, shrink):
        v = jnp.concatenate([kv[xk, 1].reshape(keys, HEAD_DIM), jnp.ones((keys, HEAD_DIM), jnp.bfloat16)], axis=1)
        total = acc[i] * shrink + jnp.dot(p, v, preferred_element_type=jnp.float32)
        if i // 2 > xk:
            acc[i] = total
        else:
            o = (total[:, :HEAD_DIM] / total[:, HEAD_DIM:]).astype(jnp.bfloat16)
            osend[i] = jnp.concatenate([o[:rows], o[rows:]], axis=1)

    def run(units):
        sc, held = scores(*units[0]), None
        for n, unit in enumerate(units):
            later = scores(*units[n + 1]) if n + 1 < len(units) else None
            p = weights(*unit, sc)
            if held is not None:
                add(*held)
            held, sc = (*unit, *p), later
        add(*held)

    def plane(xk):
        run([(xk, i) for i in range(2 * xk, BLOCKS)])
        for j in range(2):
            out_copy("start", xk, j)

    for n in range(SIDE):
        send_far(order(n))
    for i in range(BLOCKS):
        pltpu.make_async_copy(qg.at[i], qg.at[i], q_rs.at[i]).wait()
    for xk in range(SIDE):
        ready(xk)
        plane(xk)

    for h in range(KV_HEADS):
        ref = out_ref.at[:, pl.ds(h * WIDE, WIDE)]
        pltpu.make_async_copy(ref, ref, o_rs.at[h]).wait()
    first("wait", (0, 1, 2))
    for xk in range(SIDE):
        cross(xk).wait_send()
        for side in range(2):
            for turn in range(1, SIDE):
                (ring(xk, side, turn) if side or turn != 2 else pass_on(xk)).wait_send()
        for j in range(2):
            out_copy("wait", xk, j)


def shards(query_rows, key_rows, value_rows, image_starts, image_counts):
    rows = query_rows.shape[1]
    dma = pltpu.SemaphoreType.DMA
    smem = pl.BlockSpec(memory_space=pltpu.SMEM)
    hbm = pl.BlockSpec(memory_space=pltpu.HBM)
    out = pl.pallas_call(
        kernel,
        out_shape=jax.ShapeDtypeStruct((rows, HEADS * HEAD_DIM), jnp.bfloat16),
        in_specs=[smem, smem, hbm, hbm, hbm],
        out_specs=hbm,
        scratch_shapes=[
            pltpu.VMEM((BLOCKS, rows, WIDE), jnp.bfloat16),
            pltpu.VMEM((SIDE, 2, SIDE, SIDE, rows, HEAD_DIM), jnp.bfloat16),
            pltpu.VMEM((BLOCKS, rows, HEAD_DIM), jnp.int32),
            pltpu.VMEM((BLOCKS, GROUP * rows, WIDE), jnp.float32),
            pltpu.VMEM((BLOCKS, GROUP * rows, HEAD_DIM), jnp.float32),
            pltpu.VMEM((BLOCKS, rows, WIDE), jnp.bfloat16),
            dma((2, BLOCKS)), dma((2, SIDE, 2)), dma((BLOCKS,)), dma((BLOCKS,)),
            dma((SIDE,)), dma((SIDE,)), dma((2 * PLANE,)), dma((2 * PLANE,)), dma((BLOCKS,)), dma((KV_HEADS,)),
        ],
        compiler_params=pltpu.CompilerParams(collective_id=0, has_side_effects=True, vmem_limit_bytes=56 << 20),
        name="attend",
    )(image_starts, image_counts, query_rows[0], key_rows[0], value_rows[0])
    return out[None]


def solution(mesh):
    return jax.shard_map(
        shards,
        mesh=mesh,
        in_specs=(P("req", "ctx", None), P("req", "ctx", None), P("req", "ctx", None), P("req", None), P("req")),
        out_specs=P("req", "ctx", None),
        check_vma=False,
    )
```

```python
import math

import jax
import jax.numpy as jnp
from jax import lax
from jax.experimental import pallas as pl
from jax.experimental.pallas import tpu as pltpu
from jax.sharding import PartitionSpec as P

HEADS = 16
KV_HEADS = 8
HEAD_DIM = 128
IMG = 256
SIDE = 4
PLANE = SIDE * SIDE
GROUP = HEADS // KV_HEADS
WIDE = GROUP * HEAD_DIM
BLOCKS = 2 * SIDE
NEG = -1e30
MESH = pl.DeviceIdType.MESH

score_scale = 168.0 ** (-0.5)
EXP2_SCALE = score_scale * math.log2(math.e)


def kernel(starts_ref, count_ref, q_ref, k_ref, v_ref, out_ref,
           qg, kv, lim, acc, mx, osend,
           p_ss, p_rs, q_ss, q_rs, c_ss, c_rs, r_ss, r_rs, o_ss, o_rs):
    rows = q_ref.shape[0]
    maximg = starts_ref.shape[1]
    c = lax.axis_index("ctx")
    swap = lax.axis_index("req") % 2
    x, y, z = c // PLANE, (c // SIDE) % SIDE, c % SIDE
    a = x + swap * (y - x)
    s = y + swap * (x - y)
    near = 2 * (z // 2)
    far = 2 - near
    zi = z % 2
    pair = z + 1 - 2 * zi
    outer = (z + z // 2 + 1) % 2
    head = SIDE * outer + a
    is_self = (swap == 0) | (y % 2 == 0)

    def origin(xk):
        return y + swap * ((x - y - xk + 2 * SIDE) % SIDE - y)

    def chip(xx, yy, zz):
        return {"ctx": xx * PLANE + yy * SIDE + zz}

    def beside(step):
        ss = (s + step + SIDE) % SIDE
        return chip(a + swap * (ss - a), ss + swap * (a - ss), z)

    def keeper(aa, zz):
        return chip(aa + swap * ((x + y + aa) % SIDE - aa), y + swap * (aa - y), zz)

    mirror = chip(x, y, SIDE - 1 - z)

    barrier = pltpu.get_barrier_semaphore()

    def hello(to):
        pl.semaphore_signal(barrier, inc=1, device_id=to, device_id_type=MESH)

    for d in range(SIDE):
        for zz in (z, pair):
            if d == 0 and zz is z:
                @pl.when(jnp.logical_not(is_self))
                def _():
                    hello(keeper(a, z))
                    hello(chip(x, origin(x), z))
            else:
                hello(keeper((a + d) % SIDE, zz))
                xx = (x + d) % SIDE
                hello(chip(xx, origin(xx), zz))
    for step in range(1, SIDE):
        hello(beside(step))
    hello(mirror)
    pl.semaphore_wait(barrier, 5 * SIDE - 2 * is_self.astype(jnp.int32))

    def cols(n, width):
        return pl.ds(pl.multiple_of(n * width, width), width)

    def first_copies(d, m, t):
        ta = (a + d) % SIDE
        th = SIDE * ((outer + m) % 2) + ta
        to = keeper(ta, pair if m else z)
        n = (d * 2 + m)
        if t < 2:
            src = (k_ref, v_ref)[t].at[:, cols(th, HEAD_DIM)]
            return src, kv.at[x, t, y, z], p_ss.at[t, n], p_rs.at[t, x, zi], to
        return q_ref.at[:, cols(th, WIDE)], qg.at[2 * x + zi], q_ss.at[n], q_rs.at[2 * x + zi], to

    def remote(src, dst, ss, rs, to):
        return pltpu.make_async_remote_copy(src_ref=src, dst_ref=dst, send_sem=ss, recv_sem=rs, device_id=to,
                                            device_id_type=MESH)

    def first(op, ts):
        for d in (0, 3, 1, 2):
            for m in (1, 0):
                for t in ts:
                    src, dst, ss, rs, to = first_copies(d, m, t)
                    if d == 0 and m == 0:
                        if op == "start":
                            @pl.when(is_self)
                            def _():
                                pltpu.make_async_copy(src, dst, rs).start()

                        @pl.when(jnp.logical_not(is_self))
                        def _():
                            copy = remote(src, dst, ss, rs, to)
                            copy.start() if op == "start" else copy.wait_send()
                    else:
                        copy = remote(src, dst, ss, rs, to)
                        copy.start() if op == "start" else copy.wait_send()

    first("start", (0, 1))
    first("start", (2,))
    def limits(i, carry):
        pos = ((i // 2) * PLANE + origin(i // 2) * SIDE + near + i % 2) * rows + lax.broadcasted_iota(jnp.int32, (rows, HEAD_DIM), 0)
        slot = pos // IMG * IMG
        found = jnp.zeros((rows, HEAD_DIM), jnp.int32)
        for n in range(maximg):
            begin = jnp.where(n < count_ref[0], starts_ref[0, n], -1)
            found = jnp.where(slot == begin, 1, found)
        lim[i] = jnp.where(found > 0, slot + (IMG - 1), pos)
        return carry

    lax.fori_loop(0, BLOCKS, limits, 0)


    def part(xk, off, half):
        return kv.at[xk, :, (origin(xk) + off + SIDE) % SIDE, pl.ds(half, 2)]

    def cross(xk):
        return remote(part(xk, 0, near), part(xk, 0, near), c_ss.at[xk], c_rs.at[xk], mirror)

    def crossed(xk):
        remote(part(xk, 0, far), part(xk, 0, far), c_ss.at[xk], c_rs.at[xk], mirror).wait_recv()

    def ring(xk, side, step):
        ref = part(xk, 0, far if side else near)
        n = (xk * 2 + side) * SIDE + step
        return remote(ref, ref, r_ss.at[n], r_rs.at[n], beside(step))

    def ring_got(xk, side, step):
        ref = part(xk, SIDE - step, far if side else near)
        n = (xk * 2 + side) * SIDE + step
        remote(ref, ref, r_ss.at[n], r_rs.at[n], beside(step)).wait_recv()

    def send_near(xk):
        for turn in (1, 3):
            ring(xk, 0, turn).start()

    soon = x + swap * ((x - 2 * y + 2 * SIDE) % SIDE - x)

    def order(i):
        return soon if i == 0 else i - 1 + (soon <= i - 1).astype(jnp.int32)

    for i in range(SIDE):
        xk = order(i)
        for t in range(2):
            for zz in range(2):
                ref = kv.at[xk, t, origin(xk), near + zz]
                pltpu.make_async_copy(ref, ref, p_rs.at[t, xk, zz]).wait()
        cross(xk).start()
        if i < 4:
            send_near(xk)

    def pass_on(xk):
        n = xk * 2 * SIDE + 2
        ref = part(xk, SIDE - 1, near)
        return remote(ref, ref, r_ss.at[n], r_rs.at[n], beside(1))

    for xk in range(SIDE):
        ring_got(xk, 0, 1)
        pass_on(xk).start()

    def send_far(xk):
        crossed(xk)
        for turn in (1, 3, 2):
            ring(xk, 1, turn).start()

    def ready(xk):
        for turn in range(1, SIDE):
            for side in range(2):
                if side or turn > 1:
                    ring_got(xk, side, turn)

    keys = PLANE * rows

    def out_copy(op, xq, j):
        src, dst = osend.at[2 * xq + j], out_ref.at[:, cols(head, WIDE)]
        here = (xq == x) & (origin(xq) == y) & (zi == j)
        if op == "start":
            @pl.when(here)
            def _():
                pltpu.make_async_copy(src, dst, o_rs.at[head]).start()

        @pl.when(jnp.logical_not(here))
        def _():
            copy = remote(src, dst, o_ss.at[2 * xq + j], o_rs.at[head], chip(xq, origin(xq), near + j))
            copy.start() if op == "start" else copy.wait_send()

    def scores(xk, i):
        q = qg[i]
        q = jnp.concatenate([q[:, :HEAD_DIM], q[:, HEAD_DIM:]], axis=0)
        k = kv[xk, 0].reshape(keys, HEAD_DIM)
        return lax.dot_general(q, k, (((1,), (1,)), ((), ())), preferred_element_type=jnp.float32)

    def weights(xk, i, sc):
        if i // 2 == xk:
            at = lax.broadcasted_iota(jnp.int32, (1, keys), 1) + xk * keys
            row_lim = lim[i]
            sc = jnp.where(at <= jnp.concatenate([row_lim, row_lim], axis=0)[:, :1], sc, NEG)
        top = jnp.max(sc, axis=1, keepdims=True)
        if xk > 0:
            before = mx[i][:, :1]
            top = jnp.maximum(top, before)
        mx[i] = jnp.broadcast_to(top, (GROUP * rows, HEAD_DIM))
        p = jnp.exp2((sc - top) * EXP2_SCALE).astype(jnp.bfloat16)
        return p, (jnp.exp2((before - top) * EXP2_SCALE) if xk > 0 else None)

    def add(xk, i, p, shrink):
        v = jnp.concatenate([kv[xk, 1].reshape(keys, HEAD_DIM), jnp.ones((keys, HEAD_DIM), jnp.bfloat16)], axis=1)
        total = jnp.dot(p, v, preferred_element_type=jnp.float32)
        if xk > 0:
            total = acc[i] * shrink + total
        if i // 2 > xk:
            acc[i] = total
        else:
            o = (total[:, :HEAD_DIM] / total[:, HEAD_DIM:]).astype(jnp.bfloat16)
            osend[i] = jnp.concatenate([o[:rows], o[rows:]], axis=1)

    def run(units):
        sc, held = scores(*units[0]), None
        for n, unit in enumerate(units):
            later = scores(*units[n + 1]) if n + 1 < len(units) else None
            p = weights(*unit, sc)
            if held is not None:
                add(*held)
            held, sc = (*unit, *p), later
        add(*held)

    def plane(xk):
        run([(xk, i) for i in range(2 * xk, BLOCKS)])
        for j in range(2):
            out_copy("start", xk, j)

    for n in range(SIDE):
        send_far(order(n))
    for i in range(BLOCKS):
        pltpu.make_async_copy(qg.at[i], qg.at[i], q_rs.at[i]).wait()
    for xk in range(SIDE):
        ready(xk)
        plane(xk)

    for h in range(KV_HEADS):
        ref = out_ref.at[:, pl.ds(h * WIDE, WIDE)]
        pltpu.make_async_copy(ref, ref, o_rs.at[h]).wait()
    first("wait", (0, 1, 2))
    for xk in range(SIDE):
        cross(xk).wait_send()
        for side in range(2):
            for turn in range(1, SIDE):
                (ring(xk, side, turn) if side or turn != 2 else pass_on(xk)).wait_send()
        for j in range(2):
            out_copy("wait", xk, j)


def shards(query_rows, key_rows, value_rows, image_starts, image_counts):
    rows = query_rows.shape[1]
    dma = pltpu.SemaphoreType.DMA
    smem = pl.BlockSpec(memory_space=pltpu.SMEM)
    hbm = pl.BlockSpec(memory_space=pltpu.HBM)
    out = pl.pallas_call(
        kernel,
        out_shape=jax.ShapeDtypeStruct((rows, HEADS * HEAD_DIM), jnp.bfloat16),
        in_specs=[smem, smem, hbm, hbm, hbm],
        out_specs=hbm,
        scratch_shapes=[
            pltpu.VMEM((BLOCKS, rows, WIDE), jnp.bfloat16),
            pltpu.VMEM((SIDE, 2, SIDE, SIDE, rows, HEAD_DIM), jnp.bfloat16),
            pltpu.VMEM((BLOCKS, rows, HEAD_DIM), jnp.int32),
            pltpu.VMEM((BLOCKS, GROUP * rows, WIDE), jnp.float32),
            pltpu.VMEM((BLOCKS, GROUP * rows, HEAD_DIM), jnp.float32),
            pltpu.VMEM((BLOCKS, rows, WIDE), jnp.bfloat16),
            dma((2, BLOCKS)), dma((2, SIDE, 2)), dma((BLOCKS,)), dma((BLOCKS,)),
            dma((SIDE,)), dma((SIDE,)), dma((2 * PLANE,)), dma((2 * PLANE,)), dma((BLOCKS,)), dma((KV_HEADS,)),
        ],
        compiler_params=pltpu.CompilerParams(collective_id=0, has_side_effects=True, vmem_limit_bytes=56 << 20),
        name="attend",
    )(image_starts, image_counts, query_rows[0], key_rows[0], value_rows[0])
    return out[None]


def solution(mesh):
    return jax.shard_map(
        shards,
        mesh=mesh,
        in_specs=(P("req", "ctx", None), P("req", "ctx", None), P("req", "ctx", None), P("req", None), P("req")),
        out_specs=P("req", "ctx", None),
        check_vma=False,
    )
```
